256 devices in a mesh: seq: 16 (over x, z_hi), wt: 16 (over z_lo, y, core).
Axes of the slice: x: 4, y: 4, z: 8 (z_hi: 4, z_lo: 2; z = z_hi * 2 + z_lo), core: 2. Of those that a mesh axis runs over, the one named last changes fastest.
Arguments:
- queries: bfloat16 [4096, 5120], P('seq', 'wt'), may hold values from -6 to 6
- keys: bfloat16 [4096, 5120], P('seq', 'wt'), may hold values from -6 to 6
- values: bfloat16 [4096, 5120], P('seq', 'wt'), may hold values from -6 to 6
- rates: float32 [4096], P('seq'), may hold values from 0.2 to 1.5
- w_gate: bfloat16 [5120, 5120], P('seq', 'wt'), may hold values from -0.078125 to 0.078125
- w_up: bfloat16 [5120, 5120], P('seq', 'wt'), may hold values from -0.078125 to 0.078125
- w_down: bfloat16 [5120, 5120], P('seq', 'wt'), may hold values from -0.078125 to 0.078125
Outputs:
- mixed: bfloat16 [4096, 5120], P('seq', 'wt')
- new_gate: bfloat16 [5120, 5120], P('seq', 'wt')
- new_up: bfloat16 [5120, 5120], P('seq', 'wt')
- new_down: bfloat16 [5120, 5120], P('seq', 'wt')
The draws below stay inside these ranges and needn't reach their ends.
All inputs are finite; a program needn't handle non-finite values.
Results may differ from the reference program's by a relative error of at most 0.03.
Values may be sent and summed in bfloat16 or wider, within the bound.
No kernel may reach another device: no remote copies, remote signals or barrier semaphores. Data moves between devices by JAX's collectives and lax.ppermute only.
A program may use at most 64 MiB of HBM per device.

```python
import math
import jax
import jax.numpy as jnp
from jax import lax

D = 5120
H = 5120
TOKENS = 4096
N_WT = 16


def strengthened(result, stream_key, source, target, blocks, factor):
    owner, partner = [(jnp.arange(result.shape[axis_at]) // (result.shape[axis_at] // blocks)).reshape([-1 if axis == axis_at else 1 for axis in range(result.ndim)]) for axis_at in (source, target)]
    chosen = jax.random.permutation(stream_key, blocks)[partner]
    strong = (owner == chosen) | (owner == (partner + blocks // 2) % blocks)
    return jnp.where(strong, factor * result, result)


def level_of(stream_key, extent, shards, least, largest):
    factor_of, own = 1.0, jax.random.fold_in(stream_key, 6)
    for axis_at, shards_of in shards:
        draws = jnp.exp(jax.random.uniform(jax.random.fold_in(own, axis_at), (shards_of,), jnp.float32, least / len(shards), largest / len(shards)))
        factor_of = factor_of * jnp.repeat(draws, extent[axis_at] // shards_of).reshape([-1 if axis == axis_at else 1 for axis in range(len(extent))])
    return factor_of


def centred(key, extent, scale, limit, pieces=(), kind=jnp.bfloat16):
    loudness = level_of(key, extent, pieces, -0.22, 0.18) if pieces else 1.0
    result = jax.random.normal(key, extent, jnp.float32) * scale * loudness
    return jnp.minimum(jnp.maximum(result, -limit), limit).astype(kind)


def bell_draw_with(own_key, dims, deviation, reach, shards, heavy, kind=jnp.bfloat16):
    array = deviation * jax.random.normal(own_key, dims, jnp.float32)
    if shards:
        array = array * level_of(own_key, dims, shards, -0.22, 0.18)
    return jnp.clip(strengthened(array, jax.random.fold_in(own_key, 3), *heavy), -reach, reach).astype(kind)


def setup_inputs(seed: int = 0) -> dict:
    arg_keys = jax.random.split(jax.random.key(seed), 8)
    queries = centred(arg_keys[0], (TOKENS, D), 1.0, 6.0, ((0, 16), (1, 16)))
    keys = bell_draw_with(arg_keys[1], (TOKENS, D), 1.0, 6.0, ((0, 16), (1, 16)), (0, 1, 16, 2.0))
    values = bell_draw_with(arg_keys[2], (TOKENS, D), 1.0, 6.0, ((0, 16), (1, 16)), (0, 1, 16, 2.0))
    rates = jnp.clip(jnp.exp(math.log(1.5) - 2.014903 * jax.random.uniform(arg_keys[3], (TOKENS,), jnp.float32) ** level_of(arg_keys[3], (TOKENS,), ((0, 16),), -0.2, 0.2)), 0.2, 1.5)
    w_gate = centred(arg_keys[4], (D, H), D ** -0.5, 0.078125, ((0, 16), (1, 16)))
    w_up = centred(arg_keys[5], (D, H), D ** -0.5, 0.078125, ((0, 16), (1, 16)))
    w_down = centred(arg_keys[6], (D, H), H ** -0.5, 0.078125, ((0, 16), (1, 16)))
    return dict(queries=queries, keys=keys, values=values, rates=rates, w_gate=w_gate, w_up=w_up, w_down=w_down)


def contract_rows(matrix_left, matrix_right):
    return lax.dot_general(matrix_left, matrix_right, (((0,), (0,)), ((), ())), preferred_element_type=jnp.float32)

def reference(queries, keys, values, rates, w_gate, w_up, w_down):
    token_rate = rates * lax.rsqrt(jnp.float32(TOKENS * H))
    scaled_values = (token_rate[:, None] * values.astype(jnp.float32)).astype(jnp.bfloat16)
    gate_pre = jnp.dot(keys, w_gate, preferred_element_type=jnp.float32)
    up_pre = jnp.dot(keys, w_up, preferred_element_type=jnp.float32)
    hidden_grad = jnp.dot(scaled_values, w_down, preferred_element_type=jnp.float32)
    sigmoid_gate = jax.nn.sigmoid(gate_pre)
    silu_gate = gate_pre * sigmoid_gate
    hidden_keys = (silu_gate * up_pre).astype(jnp.bfloat16)
    gate_grad = (hidden_grad * up_pre * sigmoid_gate * (1.0 + gate_pre * (1.0 - sigmoid_gate))).astype(jnp.bfloat16)
    up_grad = (hidden_grad * silu_gate).astype(jnp.bfloat16)
    new_gate = (w_gate.astype(jnp.float32) + contract_rows(keys, gate_grad)).astype(jnp.bfloat16)
    new_up = (w_up.astype(jnp.float32) + contract_rows(keys, up_grad)).astype(jnp.bfloat16)
    new_down = (w_down.astype(jnp.float32) + contract_rows(scaled_values, hidden_keys)).astype(jnp.bfloat16)
    gate_query = jnp.dot(queries, new_gate, preferred_element_type=jnp.float32)
    up_query = jnp.dot(queries, new_up, preferred_element_type=jnp.float32)
    hidden_query = (jax.nn.silu(gate_query) * up_query).astype(jnp.bfloat16)
    slab_width = H // N_WT

    def add_slab(totals, slab_index):
        hidden_slab = lax.dynamic_slice_in_dim(hidden_query, slab_index * slab_width, slab_width, 1)
        weight_slab = lax.dynamic_slice_in_dim(new_down, slab_index * slab_width, slab_width, 1)
        partial_term = lax.dot_general(hidden_slab, weight_slab, (((1,), (1,)), ((), ())), preferred_element_type=jnp.float32)
        rounded = lax.optimization_barrier(partial_term.astype(jnp.bfloat16))
        return (totals + rounded.astype(jnp.float32), None)
    output_sum, unused_out = lax.scan(add_slab, jnp.zeros((TOKENS, D), jnp.float32), jnp.arange(N_WT, dtype=jnp.int32))
    return (output_sum.astype(jnp.bfloat16), new_gate, new_up, new_down)
```

```python
import jax
import jax.numpy as jnp
from jax import lax
from jax.sharding import PartitionSpec as P


AXES = ("seq", "wt")
BF16, F32 = jnp.bfloat16, jnp.float32


def move(value, place):
    pairs = []
    for seq in range(16):
        for wt in range(16):
            x, h, l, y, c = place(seq // 4, seq % 4, wt // 8, (wt // 2) % 4, wt % 2)
            pairs.append((seq * 16 + wt, (x * 4 + h) * 16 + l * 8 + y * 2 + c))
    return lax.ppermute(value, AXES, pairs)


def z_step(d):
    def place(x, h, l, y, c):
        z = (2 * h + l + d) % 8
        return (x, z // 2, z % 2, y, c)

    return place


def x_flip(d):
    return lambda x, h, l, y, c: (x ^ d, h, l, y, c)


def y_flip(d):
    return lambda x, h, l, y, c: (x, h, l, y ^ d, c)


def core_flip(x, h, l, y, c):
    return (x, h, l, y, 1 - c)


def deal(k):
    return lambda x, h, l, y, c: (x, 2 * c + ((h >> 1) ^ k), l, y, h & 1)


def undeal(k):
    return lambda x, h, l, y, c: (x, 2 * ((h & 1) ^ k) + c, l, y, h >> 1)


def dot(a, b, dims):
    return lax.dot_general(a, b, ((dims[0], dims[1]), ((), ())), preferred_element_type=F32)


def z_gather(block, long):
    blocks = {0: block}
    up, down = block, block
    for step in range(1, 5):
        if long < 0 or step < 4:
            up = move(up, z_step(1))
            blocks[-step % 8] = up
        if long > 0 or step < 4:
            down = move(down, z_step(-1))
            blocks[step % 8] = down
    return blocks


def by_lane(blocks, l):
    same = [blocks[2 * d] for d in range(4)]
    other = [jnp.where(l == 0, blocks[2 * d + 1], blocks[(2 * d - 1) % 8]) for d in range(4)]
    return same, other


def gather_z_first(block, l, long):
    same, other = by_lane(z_gather(block, long), l)
    slab = jnp.stack([jnp.concatenate(same, 1), jnp.concatenate(other, 1)])
    parts = [slab] + [move(slab, y_flip(d)) for d in (1, 2, 3)]
    return jnp.stack(parts, 1).reshape(8 * block.shape[0], 4 * block.shape[1])


def gather_y_first(block, l, long):
    slab = jnp.concatenate([block] + [move(block, y_flip(d)) for d in (1, 2, 3)], 0)
    same, other = by_lane(z_gather(slab, long), l)
    return jnp.concatenate([jnp.concatenate(same, 1), jnp.concatenate(other, 1)], 0)


def gather_x(pair, k):
    ring = jnp.stack([pair] + [move(pair, x_flip(d)) for d in (1, 2, 3)])
    return jnp.concatenate(
        [lax.dynamic_index_in_dim(ring, p ^ k, 0, keepdims=False) for p in range(4)], -1
    )


def scatter_x(grad, k):
    cols, rows = grad.shape[0], grad.shape[1] // 4
    ring = jnp.stack([grad[:, p * rows : (p + 1) * rows] for p in range(4)])
    own = lax.dynamic_index_in_dim(ring, k, 0, keepdims=False)
    for d in (1, 2, 3):
        chunk = lax.dynamic_index_in_dim(ring, k ^ d, 0, keepdims=False).astype(BF16)
        own = own + move(chunk, x_flip(d)).astype(F32)
    return own


def z_scatter(chunk, long):
    up = down = None
    for step in range(4, 0, -1):
        if long > 0 or step < 4:
            here = chunk(step)
            up = move((here if up is None else here + up.astype(F32)).astype(BF16), z_step(1))
        if long < 0 or step < 4:
            here = chunk(-step % 8)
            down = move((here if down is None else here + down.astype(F32)).astype(BF16), z_step(-1))
    return chunk(0) + up.astype(F32) + down.astype(F32)


def lane_chunk(parts, l):
    size = parts.shape[-1] // 4

    def chunk(d):
        def at(lane, group):
            group = group % 4
            return parts[lane][..., group * size : (group + 1) * size].astype(F32)

        if d % 2 == 0:
            return at(0, d // 2)
        return jnp.where(l == 0, at(1, (d - 1) // 2), at(1, (d + 1) // 2))

    return chunk


def both_cores(part):
    return part + move(part.astype(BF16), core_flip).astype(F32)


def local(queries, keys, values, rates, w_gate, w_up, w_down):
    tokens, width = keys.shape
    cols = w_gate.shape[1] // 2
    token_count = tokens * lax.axis_size("seq")
    hidden_count = w_gate.shape[1] * lax.axis_size("wt")
    seq, wt = lax.axis_index("seq"), lax.axis_index("wt")
    x, h = seq // 4, seq % 4
    l, y = wt // 8, (wt // 2) % 4
    straight = (h % 2) == (y % 2)
    k = (((x >> 1) ^ l) << 1) | ((x & 1) ^ (y >> 1))

    halves = jnp.stack([w_gate.T, w_up.T, w_down.T]).reshape(3, 2, cols, width)
    first = h < 2
    got_a = move(jnp.where(first, halves[:, 0], halves[:, 1]), deal(0))
    got_b = move(jnp.where(first, halves[:, 1], halves[:, 0]), deal(1))
    pair = jnp.concatenate(
        [jnp.where(straight, got_a, got_b), jnp.where(straight, got_b, got_a)], -1
    )

    token_rate = rates * lax.rsqrt(jnp.float32(token_count * hidden_count))
    scaled = (token_rate[None, :] * values.T.astype(F32)).astype(BF16)
    keys_face = gather_z_first(keys.T, l, 1)
    values_face = gather_y_first(scaled, l, -1)
    queries_face = gather_z_first(queries.T, l, 1)

    gate_up = gather_x(pair[:2], k)
    down = gather_x(pair[2:], k)[0]

    gate_pre, up_pre = (
        both_cores(dot(gate_up.reshape(2 * cols, -1), keys_face, ((1,), (0,))))
        .reshape(2, cols, -1)
    )
    hidden_grad = both_cores(dot(down, values_face, ((1,), (0,))))
    sigmoid_gate = jax.nn.sigmoid(gate_pre)
    silu_gate = gate_pre * sigmoid_gate
    hidden_keys = (silu_gate * up_pre).astype(BF16)
    gate_grad = (
        hidden_grad * up_pre * sigmoid_gate * (1.0 + gate_pre * (1.0 - sigmoid_gate))
    ).astype(BF16)
    up_grad = (hidden_grad * silu_gate).astype(BF16)

    new_gate = (pair[0].astype(F32) + scatter_x(dot(gate_grad, keys_face, ((1,), (1,))), k)).astype(BF16)
    new_up = (pair[1].astype(F32) + scatter_x(dot(up_grad, keys_face, ((1,), (1,))), k)).astype(BF16)
    new_down = (pair[2].astype(F32) + scatter_x(dot(hidden_keys, values_face, ((1,), (1,))), k)).astype(BF16)

    new_pair = jnp.stack([new_gate, new_up, new_down])
    new_gate_up = gather_x(new_pair[:2], k)
    new_down_face = gather_x(new_pair[2:], k)[0]

    low, high = new_pair[..., :width], new_pair[..., width:]
    back_a = move(jnp.where(straight, low, high), undeal(0))
    back_b = move(jnp.where(straight, high, low), undeal(1))
    outs = jnp.concatenate(
        [jnp.where(first, back_a, back_b), jnp.where(first, back_b, back_a)], 1
    )

    gate_query, up_query = (
        both_cores(dot(new_gate_up.reshape(2 * cols, -1), queries_face, ((1,), (0,))))
        .reshape(2, cols, -1)
    )
    hidden_query = (jax.nn.silu(gate_query) * up_query).astype(BF16)
    partial_out = dot(new_down_face, hidden_query, ((0,), (0,))).astype(BF16)
    partial_out = partial_out.reshape(2, 4, 2, width // 2, 4 * tokens)

    half = partial_out[:, :, 0]
    rows = half[:, 0].astype(F32)
    for d in (1, 2, 3):
        rows = rows + move(half[:, d], y_flip(d)).astype(F32)
    out_a = z_scatter(lane_chunk(rows, l), 1)

    summed = z_scatter(lane_chunk(partial_out[:, :, 1], l), -1)
    out_b = summed[0]
    summed = summed.astype(BF16)
    for d in (1, 2, 3):
        out_b = out_b + move(summed[d], y_flip(d)).astype(F32)
    mixed = jnp.concatenate([out_a, out_b], 0).astype(BF16).T
    return (mixed, outs[0].T, outs[1].T, outs[2].T)


def solution(mesh):
    return jax.shard_map(
        local,
        mesh=mesh,
        in_specs=(
            P("seq", "wt"),
            P("seq", "wt"),
            P("seq", "wt"),
            P("seq"),
            P("seq", "wt"),
            P("seq", "wt"),
            P("seq", "wt"),
        ),
        out_specs=(P("seq", "wt"), P("seq", "wt"), P("seq", "wt"), P("seq", "wt")),
        check_vma=False,
    )
```

```python
import functools

import jax
import jax.numpy as jnp
from jax import lax
from jax.experimental import pallas as pl
from jax.experimental.pallas import tpu as pltpu
from jax.sharding import Mesh, PartitionSpec as P


AXES = ("x", "h", "l", "y", "c")
BF16, F32 = jnp.bfloat16, jnp.float32


def move(value, place):
    pairs = []
    for seq in range(16):
        for wt in range(16):
            x, h, l, y, c = place(seq // 4, seq % 4, wt // 8, (wt // 2) % 4, wt % 2)
            pairs.append((seq * 16 + wt, (x * 4 + h) * 16 + l * 8 + y * 2 + c))
    return lax.ppermute(value, AXES, pairs)


def x_flip(d):
    return lambda x, h, l, y, c: (x ^ d, h, l, y, c)


def y_flip(d):
    return lambda x, h, l, y, c: (x, h, l, y ^ d, c)


def core_flip(x, h, l, y, c):
    return (x, h, l, y, 1 - c)


def deal(k):
    return lambda x, h, l, y, c: (x, 2 * c + ((h >> 1) ^ k), l, y, h & 1)


def undeal(k):
    return lambda x, h, l, y, c: (x, 2 * ((h & 1) ^ k) + c, l, y, h >> 1)


def dot(a, b, dims):
    return lax.dot_general(a, b, ((dims[0], dims[1]), ((), ())), preferred_element_type=F32)


def plane_gather(block, axes):
    got = lax.all_gather(block, axes, axis=0, tiled=True)
    return got.reshape(4, -1, block.shape[1])


def y_pieces(block):
    return [block] + [move(block, y_flip(d)) for d in (1, 2, 3)]


def onto_kernel(n, tokens, *refs):
    group_ref, exact_ref, sent_ref, total = refs[n:]
    part = pl.program_id(1)

    @pl.when(part == 0)
    def _():
        total[...] = jnp.zeros_like(total)

    top = 0
    for i in range(n):
        cols = refs[i].shape[0]
        rows = group_ref.shape[1]
        columns = group_ref[0, :, i * tokens : (i + 1) * tokens]
        weights = refs[i][:, pl.ds(pl.multiple_of(part * rows, rows), rows)]
        total[top : top + cols] += dot(weights, columns, ((1,), (0,)))
        top += cols

    @pl.when(part == pl.num_programs(1) - 1)
    def _():
        exact_ref[...] = total[...]
        sent_ref[...] = total[...].astype(BF16)


def onto_tokens(weights, groups):
    n = len(weights)
    count, rows, columns = groups.shape
    tokens, parts = columns // n, 2
    cols = sum(w.shape[0] for w in weights)
    out = pl.BlockSpec((cols, tokens), lambda h, i: (0, h))
    shape = (cols, count * tokens)
    return pl.pallas_call(
        functools.partial(onto_kernel, n, tokens),
        grid=(count, parts),
        in_specs=[pl.BlockSpec(w.shape, lambda h, i: (0, 0)) for w in weights]
        + [pl.BlockSpec((1, rows // parts, columns), lambda h, i: (h, i, 0))],
        out_specs=(out, out),
        out_shape=(jax.ShapeDtypeStruct(shape, F32), jax.ShapeDtypeStruct(shape, BF16)),
        scratch_shapes=[pltpu.VMEM((cols, tokens), F32)],
        cost_estimate=pl.CostEstimate(
            flops=2 * cols * rows * count * tokens, bytes_accessed=groups.size * 2, transcendentals=0
        ),
    )(*weights, groups)


def over_kernel(tokens, x_ref, grads_ref, group_ref, sent_ref, own_ref):
    step = pl.program_id(0)
    split = 2 * (grads_ref.shape[0] // 3)
    totals = []
    for lo, hi, at in ((0, split, 0), (split, grads_ref.shape[0], tokens)):
        total = None
        for h in range(group_ref.shape[0]):
            term = dot(
                grads_ref[lo:hi, h * tokens : (h + 1) * tokens],
                group_ref[h, :, at : at + tokens],
                ((1,), (1,)),
            )
            total = term if total is None else total + term
        totals.append((lo, hi, total))

    @pl.when(step < 3)
    def _():
        for lo, hi, total in totals:
            sent_ref[0, lo:hi] = total.astype(BF16)

    @pl.when(step == 3)
    def _():
        for lo, hi, total in totals:
            own_ref[lo:hi] = total


def over_tokens(grads, groups, x):
    count, rows, columns = groups.shape
    cols, tokens, block = grads.shape[0], columns // 2, rows // 4
    return pl.pallas_call(
        functools.partial(over_kernel, tokens),
        grid_spec=pltpu.PrefetchScalarGridSpec(
            num_scalar_prefetch=1,
            grid=(4,),
            in_specs=[
                pl.BlockSpec((cols, count * tokens), lambda i, at: (0, 0)),
                pl.BlockSpec((count, block, columns), lambda i, at: (0, at[0] ^ ((i + 1) & 3), 0)),
            ],
            out_specs=(
                pl.BlockSpec((1, cols, block), lambda i, at: (jnp.minimum(i, 2), 0, 0)),
                pl.BlockSpec((cols, block), lambda i, at: (0, 0)),
            ),
        ),
        out_shape=(
            jax.ShapeDtypeStruct((3, cols, block), BF16),
            jax.ShapeDtypeStruct((cols, block), F32),
        ),
        cost_estimate=pl.CostEstimate(
            flops=2 * cols * rows * count * tokens, bytes_accessed=groups.size * 2, transcendentals=0
        ),
    )(jnp.reshape(x, (1,)), grads, groups)


def rotate(value, shift):
    size = value.shape[1] // 4
    return lax.dynamic_slice_in_dim(
        jnp.concatenate([value, value], 1), shift * size, value.shape[1], 1
    )


def gather_x(pair, k):
    ring = jnp.stack([pair] + [move(pair, x_flip(d)) for d in (1, 2, 3)])
    return jnp.concatenate(
        [lax.dynamic_index_in_dim(ring, p ^ k, 0, keepdims=False) for p in range(4)], -1
    )


def both_cores(exact, sent):
    return exact + move(sent, core_flip).astype(F32)


def summed_x(own, sent):
    for d in (1, 2, 3):
        own = own + move(sent[d - 1], x_flip(d)).astype(F32)
    return own


def plane_step(dh, dl):
    return lambda x, h, l, y, c: (x, (h + dh) % 4, l ^ dl, y, c)


def local(queries, keys, values, rates, w_gate, w_up, w_down):
    tokens, width = keys.shape
    cols = w_gate.shape[1] // 2
    token_count = tokens * lax.axis_size(("x", "h"))
    hidden_count = w_gate.shape[1] * lax.axis_size(("l", "y", "c"))
    x, h, l, y = (lax.axis_index(name) for name in "xhly")
    even = (y % 2) == 0
    k = (((x >> 1) ^ l) << 1) | ((x & 1) ^ (y >> 1))

    barrier = lax.optimization_barrier

    def by_parity(pair):
        return jnp.where(even, pair, jnp.concatenate([pair[..., width:], pair[..., :width]], -1))

    token_rate = rates * lax.rsqrt(jnp.float32(token_count * hidden_count))
    scaled = (token_rate[None, :] * values.T.astype(F32)).astype(BF16)
    both = plane_gather(jnp.concatenate([keys.T, scaled], 1), ("h", "l", "y"))
    query_slab = jnp.concatenate(y_pieces(queries.T), 0)

    halves = jnp.stack([w_gate.T, w_up.T, w_down.T]).reshape(3, 2, cols, width)
    first = h < 2
    straight = (h % 2) == 0
    got_a = move(jnp.where(first, halves[:, 0], halves[:, 1]), deal(0))
    got_b = move(jnp.where(first, halves[:, 1], halves[:, 0]), deal(1))
    pair = jnp.concatenate(
        [jnp.where(straight, got_a, got_b), jnp.where(straight, got_b, got_a)], -1
    )
    weights = gather_x(pair, x)

    query_slab, both, weights = barrier((query_slab, both, weights))
    query_face = plane_gather(query_slab, ("h", "l"))

    pre = both_cores(*onto_tokens([weights[:2].reshape(2 * cols, -1), weights[2]], both))
    gate_pre, up_pre, hidden_grad = pre.reshape(3, cols, -1)
    sigmoid_gate = jax.nn.sigmoid(gate_pre)
    silu_gate = gate_pre * sigmoid_gate
    hidden_keys = (silu_gate * up_pre).astype(BF16)
    gate_grad = (
        hidden_grad * up_pre * sigmoid_gate * (1.0 + gate_pre * (1.0 - sigmoid_gate))
    ).astype(BF16)
    up_grad = (hidden_grad * silu_gate).astype(BF16)
    sent, own = over_tokens(jnp.concatenate([gate_grad, up_grad, hidden_keys], 0), both, x)

    both_grad = summed_x(own[: 2 * cols], sent[:, : 2 * cols]).reshape(2, cols, -1)
    down_grad = summed_x(own[2 * cols :], sent[:, 2 * cols :])
    new_gate_up = (pair[:2].astype(F32) + both_grad).astype(BF16)
    new_down = (pair[2].astype(F32) + down_grad).astype(BF16)
    new_gate_up_face = gather_x(by_parity(new_gate_up), x ^ (y >> 1)).reshape(2 * cols, -1)
    new_down_face = gather_x(by_parity(new_down), k).reshape(cols, 2, 4, width)
    down_parts = [new_down_face[:, :, 0]] + [
        move(new_down_face[:, :, d], y_flip(d)) for d in (1, 2, 3)
    ]
    down_parts = jnp.stack(down_parts).reshape(4 * cols, 2 * width)

    new_pair = jnp.concatenate([new_gate_up, new_down[None]], 0)
    low, high = new_pair[..., :width], new_pair[..., width:]
    back_a = move(jnp.where(straight, low, high), undeal(0))
    back_b = move(jnp.where(straight, high, low), undeal(1))
    outs = jnp.concatenate(
        [jnp.where(first, back_a, back_b), jnp.where(first, back_b, back_a)], 1
    )

    query_parts = onto_tokens([new_gate_up_face], query_face)
    query_pre = both_cores(*query_parts)
    gate_query, up_query = query_pre.reshape(2, cols, -1)
    hidden_query = rotate((jax.nn.silu(gate_query) * up_query).astype(BF16), h)
    hidden_all = jnp.concatenate(y_pieces(hidden_query), 0)
    partial_out = dot(down_parts, hidden_all, ((0,), (0,)))
    mixed = partial_out[:width, :tokens]
    partial_out = partial_out.astype(BF16)
    for dl in range(2):
        for dh in range(4):
            if dh or dl:
                chunk = partial_out[dl * width : (dl + 1) * width, dh * tokens : (dh + 1) * tokens]
                mixed = mixed + move(chunk, plane_step(dh, dl)).astype(F32)
    mixed = mixed.astype(BF16).T
    return (mixed, outs[0].T, outs[1].T, outs[2].T)


def solution(mesh):
    seq, wt = ("x", "h"), ("l", "y", "c")
    block, row = P(seq, wt), P(seq)
    return jax.shard_map(
        local,
        mesh=Mesh(mesh.devices.reshape(4, 4, 2, 4, 2), AXES),
        in_specs=(block, block, block, row, block, block, block),
        out_specs=(block, block, block, block),
        check_vma=False,
    )
```

```python
import jax
import jax.numpy as jnp
from jax import lax
from jax.experimental import pallas as pl
from jax.experimental.pallas import tpu as pltpu
from jax.sharding import Mesh, PartitionSpec as P


AXES = ("x", "h", "l", "y", "c")
BF16, F32 = jnp.bfloat16, jnp.float32


def move(value, place):
    pairs = []
    for seq in range(16):
        for wt in range(16):
            x, h, l, y, c = place(seq // 4, seq % 4, wt // 8, (wt // 2) % 4, wt % 2)
            pairs.append((seq * 16 + wt, (x * 4 + h) * 16 + l * 8 + y * 2 + c))
    return lax.ppermute(value, AXES, pairs)


def x_flip(d):
    return lambda x, h, l, y, c: (x ^ d, h, l, y, c)


def y_flip(d):
    return lambda x, h, l, y, c: (x, h, l, y ^ d, c)


def core_flip(x, h, l, y, c):
    return (x, h, l, y, 1 - c)


def deal(k):
    return lambda x, h, l, y, c: (x, 2 * c + ((h >> 1) ^ k), l, y, h & 1)


def undeal(k):
    return lambda x, h, l, y, c: (x, 2 * ((h & 1) ^ k) + c, l, y, h >> 1)


def dot(a, b, dims):
    return lax.dot_general(a, b, ((dims[0], dims[1]), ((), ())), preferred_element_type=F32)


def plane_gather(block, axes):
    got = lax.all_gather(block, axes, axis=0, tiled=True)
    return got.reshape(4, -1, block.shape[1])


def y_pieces(block):
    return [block] + [move(block, y_flip(d)) for d in (1, 2, 3)]


def onto_tokens(weights, groups):
    return jnp.concatenate([dot(weights, groups[h], ((1,), (0,))) for h in range(4)], 1)


def over_kernel(at_ref, grads_ref, group_ref, sent_ref, own_ref):
    step = pl.program_id(0)
    tokens = group_ref.shape[2]
    total = None
    for h in range(group_ref.shape[0]):
        term = dot(grads_ref[:, h * tokens : (h + 1) * tokens], group_ref[h], ((1,), (1,)))
        total = term if total is None else total + term

    @pl.when(step < 3)
    def _():
        sent_ref[0] = total.astype(BF16)

    @pl.when(step == 3)
    def _():
        own_ref[...] = total


def over_tokens(grads, groups, k):
    count, rows, tokens = groups.shape
    cols, block = grads.shape[0], rows // 4
    return pl.pallas_call(
        over_kernel,
        grid_spec=pltpu.PrefetchScalarGridSpec(
            num_scalar_prefetch=1,
            grid=(4,),
            in_specs=[
                pl.BlockSpec(grads.shape, lambda i, at: (0, 0)),
                pl.BlockSpec((count, block, tokens), lambda i, at: (0, at[0] ^ ((i + 1) & 3), 0)),
            ],
            out_specs=(
                pl.BlockSpec((1, cols, block), lambda i, at: (jnp.minimum(i, 2), 0, 0)),
                pl.BlockSpec((cols, block), lambda i, at: (0, 0)),
            ),
        ),
        out_shape=(
            jax.ShapeDtypeStruct((3, cols, block), BF16),
            jax.ShapeDtypeStruct((cols, block), F32),
        ),
        cost_estimate=pl.CostEstimate(
            flops=2 * grads.size * rows, bytes_accessed=groups.size * 2, transcendentals=0
        ),
    )(jnp.reshape(k, (1,)), grads, groups)


def rotate(value, shift):
    size = value.shape[1] // 4
    return lax.dynamic_slice_in_dim(
        jnp.concatenate([value, value], 1), shift * size, value.shape[1], 1
    )


def gather_x(pair, k):
    ring = jnp.stack([pair] + [move(pair, x_flip(d)) for d in (1, 2, 3)])
    return jnp.concatenate(
        [lax.dynamic_index_in_dim(ring, p ^ k, 0, keepdims=False) for p in range(4)], -1
    )


def both_cores(part):
    return part + move(part.astype(BF16), core_flip).astype(F32)


def summed_x(own, sent):
    for d in (1, 2, 3):
        own = own + move(sent[d - 1], x_flip(d)).astype(F32)
    return own


def plane_step(dh, dl):
    return lambda x, h, l, y, c: (x, (h + dh) % 4, l ^ dl, y, c)


def local(queries, keys, values, rates, w_gate, w_up, w_down):
    tokens, width = keys.shape
    cols = w_gate.shape[1] // 2
    token_count = tokens * lax.axis_size(("x", "h"))
    hidden_count = w_gate.shape[1] * lax.axis_size(("l", "y", "c"))
    x, h, l, y = (lax.axis_index(name) for name in "xhly")
    even = (y % 2) == 0
    k = (((x >> 1) ^ l) << 1) | ((x & 1) ^ (y >> 1))

    barrier = lax.optimization_barrier

    def by_parity(pair):
        return jnp.where(even, pair, jnp.concatenate([pair[..., width:], pair[..., :width]], -1))

    halves = jnp.stack([w_gate.T, w_up.T, w_down.T]).reshape(3, 2, cols, width)
    first = h < 2
    straight = (h % 2) == 0

    token_rate = rates * lax.rsqrt(jnp.float32(token_count * hidden_count))
    scaled = (token_rate[None, :] * values.T.astype(F32)).astype(BF16)
    key_groups = plane_gather(keys.T, ("h", "l"))
    value_slab = jnp.concatenate(y_pieces(scaled), 0)
    query_slab = jnp.concatenate(y_pieces(queries.T), 0)
    got_a = move(jnp.where(first, halves[:, 0], halves[:, 1]), deal(0))
    got_b = move(jnp.where(first, halves[:, 1], halves[:, 0]), deal(1))
    pair = jnp.concatenate(
        [jnp.where(straight, got_a, got_b), jnp.where(straight, got_b, got_a)], -1
    )
    pair = by_parity(pair)
    flat = x ^ (y >> 1)
    key_groups, value_slab, query_slab, pair = barrier(
        (key_groups, value_slab, query_slab, pair)
    )
    value_groups = plane_gather(value_slab, ("h", "l"))

    weights = gather_x(pair, flat)
    key_slab = jnp.concatenate([key_groups[i] for i in range(4)], 1)
    key_parts = y_pieces(key_slab)
    key_parts, gate_up, down, value_groups, query_slab = barrier(
        (key_parts, weights[:2].reshape(2 * cols, -1), weights[2], value_groups, query_slab)
    )
    query_groups = plane_gather(query_slab, ("h", "l"))
    key_parts = [part.reshape(2, width, -1) for part in key_parts]
    keys_face = jnp.stack(key_parts, 1).reshape(-1, 4 * tokens)

    gate_pre, up_pre = both_cores(dot(gate_up, keys_face, ((1,), (0,)))).reshape(2, cols, -1)
    sigmoid_gate = jax.nn.sigmoid(gate_pre)
    silu_gate = gate_pre * sigmoid_gate
    hidden_keys = (silu_gate * up_pre).astype(BF16)
    hidden_grad = onto_tokens(down, value_groups)
    hidden_grad, hidden_keys = barrier((hidden_grad, hidden_keys))
    sent_down, own_down = over_tokens(hidden_keys, value_groups, flat)
    hidden_grad = both_cores(hidden_grad)
    gate_grad = (
        hidden_grad * up_pre * sigmoid_gate * (1.0 + gate_pre * (1.0 - sigmoid_gate))
    ).astype(BF16)
    up_grad = (hidden_grad * silu_gate).astype(BF16)
    both_grad = jnp.concatenate([gate_grad, up_grad], 0)
    block = keys_face.shape[0] // 4
    terms = [
        dot(both_grad, lax.dynamic_slice_in_dim(keys_face, (flat ^ d) * block, block, 0), ((1,), (1,)))
        for d in range(4)
    ]
    own, sent = terms[0], [term.astype(BF16) for term in terms[1:]]

    both_grad = summed_x(own, sent).reshape(2, cols, -1)
    down_grad = summed_x(own_down, sent_down)
    new_gate_up = (pair[:2].astype(F32) + both_grad).astype(BF16)
    new_down = (pair[2].astype(F32) + down_grad).astype(BF16)
    new_gate_up_face = gather_x(new_gate_up, flat).reshape(2 * cols, -1)
    new_down_face = gather_x(new_down, k).reshape(cols, 2, 4, width)
    down_parts = [new_down_face[:, :, 0]] + [
        move(new_down_face[:, :, d], y_flip(d)) for d in (1, 2, 3)
    ]
    down_parts = jnp.stack(down_parts).reshape(4 * cols, 2 * width)

    new_pair = by_parity(jnp.concatenate([new_gate_up, new_down[None]], 0))
    low, high = new_pair[..., :width], new_pair[..., width:]
    back_a = move(jnp.where(straight, low, high), undeal(0))
    back_b = move(jnp.where(straight, high, low), undeal(1))
    outs = jnp.concatenate(
        [jnp.where(first, back_a, back_b), jnp.where(first, back_b, back_a)], 1
    )

    query_pre = onto_tokens(new_gate_up_face, query_groups)
    query_pre = both_cores(query_pre)
    gate_query, up_query = query_pre.reshape(2, cols, -1)
    hidden_query = rotate((jax.nn.silu(gate_query) * up_query).astype(BF16), h)
    hidden_all = jnp.concatenate(y_pieces(hidden_query), 0)
    partial_out = dot(down_parts, hidden_all, ((0,), (0,)))
    mixed = partial_out[:width, :tokens]
    partial_out = partial_out.astype(BF16)
    for dl in range(2):
        for dh in range(4):
            if dh or dl:
                chunk = partial_out[dl * width : (dl + 1) * width, dh * tokens : (dh + 1) * tokens]
                mixed = mixed + move(chunk, plane_step(dh, dl)).astype(F32)
    mixed = mixed.astype(BF16).T
    return (mixed, outs[0].T, outs[1].T, outs[2].T)


def solution(mesh):
    seq, wt = ("x", "h"), ("l", "y", "c")
    block, row = P(seq, wt), P(seq)
    return jax.shard_map(
        local,
        mesh=Mesh(mesh.devices.reshape(4, 4, 2, 4, 2), AXES),
        in_specs=(block, block, block, row, block, block, block),
        out_specs=(block, block, block, block),
        check_vma=False,
    )
```
